1024 devices in a mesh: img: 16 (over y, core), seq: 64 (over x, z).
Axes of the slice: x: 8, y: 8, z: 8, core: 2. Of those that a mesh axis runs over, the one named last changes fastest.
Arguments:
- llm_grads: bfloat16 [16, 2048, 8192], P('img', 'seq'), may hold values from -6 to 6
- token_target: int32 [16, 2048], P('img', 'seq'), may hold values from 0 to 2047, as said below
- patches: bfloat16 [16, 8192, 1280], P('img', 'seq'), may hold values from -150 to 150
- gain: float32 [1280], replicated, may hold values from 0.5 to 1.5
- w_down: bfloat16 [5120, 8192], P(None, 'img'), may hold values from -0.078125 to 0.078125
- queries: bfloat16 [16, 8192, 1280], P('img', 'seq'), may hold values from -40 to 40
- keys: bfloat16 [16, 8192, 1280], P('img', 'seq'), may hold values from -5 to 5
- values: bfloat16 [16, 8192, 1280], P('img', 'seq'), may hold values from -5 to 5
- window_ids: int32 [16, 64, 32], P('img', 'seq'), may hold values from 0 to 3, never falling along the last dimension, each value on 1 to 16 neighbouring positions
Outputs:
- grad_q: bfloat16 [16, 8192, 1280], P('img', 'seq')
- grad_k: bfloat16 [16, 8192, 1280], P('img', 'seq')
- grad_v: bfloat16 [16, 8192, 1280], P('img', 'seq')
- gain_grad: float32 [1280], replicated
- bias_grad: float32 [8192], replicated
The draws below stay inside these ranges and needn't reach their ends.
Inputs may be any that keep to these rules, and one draw needn't show every extreme that they name: In each group i, token_target[i] is a permutation: position s * 32 + j (held by index s of seq) holds merged token d * 32 + m (held by index d of seq). At most 1 position of one seq index holds a merged token of any one seq index, and in every group some pair of seq indices has exactly 1.
All inputs are finite; a program needn't handle non-finite values.
Results may differ from the reference program's by a relative error of at most 0.024.
Values may be sent and summed in bfloat16 or wider, within the bound.
A program may use at most 64 MiB of HBM per device.

```python
import math
import jax
import jax.numpy as jnp
import numpy as np
from jax import lax

HEADS = 16
HEAD_DIM = 80
D = 1280
MERGE_IN = 5120
OUT = 8192
M_DEV = 32
P_DEV = 128
TOK_GROUP = 2048
PATCH_GROUP = 8192
CAP = 1
WIN = 16
N_IMG = 16
N_SEQ = 64


def group_tables(group_key):
    subkeys = jax.random.split(group_key, 4 + CAP)
    sigma_perm = jax.random.permutation(subkeys[0], N_SEQ).astype(jnp.int32)
    shuffle_dest = jax.random.permutation(subkeys[1], N_SEQ).astype(jnp.int32)
    window_len = M_DEV // CAP
    counts = jnp.zeros((N_SEQ, N_SEQ), jnp.int32)
    for offset in range(CAP):
        others = jax.random.permutation(subkeys[4 + offset], N_SEQ - 1).astype(jnp.int32) + 1
        mapping = jnp.concatenate([jnp.zeros((1,), jnp.int32), others])
        shifted = sigma_perm[mapping]
        counts = counts + (jnp.mod(shuffle_dest[None, :] - shifted[:, None], N_SEQ) < window_len).astype(jnp.int32)
    bounds = jnp.cumsum(counts, axis=1)
    row_ids = jnp.arange(M_DEV, dtype=jnp.int32)
    sorted_dest = jnp.sum((bounds[:, None, :] <= row_ids[None, :, None]).astype(jnp.int32), axis=2)
    row_perms = jax.vmap(lambda random_key: jax.random.permutation(random_key, M_DEV))(jax.random.split(subkeys[2], N_SEQ)).astype(jnp.int32)
    dest_of = jnp.take_along_axis(sorted_dest, row_perms, axis=1)
    flat_dest = dest_of.reshape(-1)
    ordering = jnp.argsort(flat_dest, stable=True).astype(jnp.int32)
    dest_sorted = flat_dest[ordering]
    rank_in_dest = jnp.arange(N_SEQ * M_DEV, dtype=jnp.int32) - dest_sorted * M_DEV
    slot_perms = jax.vmap(lambda random_key: jax.random.permutation(random_key, M_DEV))(jax.random.split(subkeys[3], N_SEQ)).astype(jnp.int32)
    merged_row = slot_perms[dest_sorted, rank_in_dest]
    merged_index = dest_sorted * M_DEV + merged_row
    targets = jnp.zeros((N_SEQ * M_DEV,), jnp.int32).at[ordering].set(merged_index)
    return targets


def draw_token_target(key, part):
    base_key = jax.random.fold_in(key, 4242)
    group_keys = jax.random.split(base_key, N_IMG)
    return jax.vmap(group_tables)(group_keys)


def draw_patches(key, part):
    subkeys = jax.random.split(jax.random.fold_in(key, 11), 3)
    shape = (N_IMG, PATCH_GROUP, D)
    column_scale = jnp.exp(jax.random.uniform(subkeys[2], (D,), jnp.float32, math.log(0.3), math.log(3.0)))
    base_values = jnp.clip(jax.random.normal(subkeys[0], shape, jnp.float32), -5.0, 5.0)
    row_scale = jnp.exp(jax.random.uniform(subkeys[1], (N_IMG, PATCH_GROUP, 1), jnp.float32, 0.0, math.log(10.0)))
    return (base_values * row_scale * column_scale[None, None, :]).astype(jnp.bfloat16)


def attention_pair(key):
    subkeys = jax.random.split(jax.random.fold_in(key, 23), 2)
    shape = (N_IMG, PATCH_GROUP, D)
    key_rows = jnp.clip(jax.random.normal(subkeys[0], shape, jnp.float32), -5.0, 5.0)
    query_rows = jnp.clip(jax.random.normal(subkeys[1], shape, jnp.float32), -5.0, 5.0)
    return (query_rows, key_rows)


def draw_queries(key, part):
    return attention_pair(key)[0].astype(jnp.bfloat16)


def draw_keys(key, part):
    return attention_pair(key)[1].astype(jnp.bfloat16)


def shard_levels(stream_key, shape, cuts, low, largest):
    level = 1.0
    for axis_at, parts in cuts:
        draws = jax.random.uniform(jax.random.fold_in(jax.random.fold_in(stream_key, 6), axis_at), (parts,), jnp.float32, low / len(cuts), largest / len(cuts))
        level = level * jnp.repeat(jnp.exp(draws), shape[axis_at] // parts).reshape((-1,) + (1,) * (len(shape) - 1 - axis_at))
    return level


def length_profile(count, total, limit, lean):
    loads = [(1 << 20) // math.isqrt(rank ** lean) + 1 for rank in range(2, count + 1)]
    spare, given = total - limit - (count - 1), [1] * (count - 1)
    while spare > 0:
        free = [i for i in range(count - 1) if given[i] < limit]
        whole, left = sum([loads[i] for i in free]), spare
        for i in free:
            addition = min(limit - given[i], max(1, left * loads[i] // whole), spare)
            given[i] = given[i] + addition
            spare = spare - addition
    return np.array([limit] + given)


def uneven_parts(key, count, total, most, skew):
    if count == 2:
        one = jax.random.randint(key, (), max(1, total - most), min(most, total - 1) + 1)
        return jnp.stack([one, total - one])
    sizes = jnp.asarray(length_profile(count, total, most, skew), jnp.int32)
    twos = (count - 1) // 2
    donor, taker = sizes[1:1 + 2 * twos:2], sizes[2:2 + 2 * twos:2]
    slack = jnp.minimum(donor - 1, most - taker)
    moved = jax.random.randint(jax.random.fold_in(key, 1), (twos,), 0, 1 << 20) % (slack + 1)
    sizes = sizes.at[1:1 + 2 * twos:2].set(donor - moved).at[2:2 + 2 * twos:2].set(taker + moved)
    return sizes[jax.random.permutation(jax.random.fold_in(key, 2), count)]


def centred(rng, shape, spread, reach, shards=(), held_as=jnp.bfloat16):
    array = jax.random.normal(rng, shape, jnp.float32) * spread
    if len(shards) > 0:
        array = shard_levels(rng, shape, shards, -0.22, 0.18) * array
    return jnp.clip(array, min=-reach, max=reach).astype(held_as)


def setup_inputs(seed: int = 0) -> dict:
    splits = jax.random.split(jax.random.key(seed), 10)
    llm_grads = centred(splits[0], (N_IMG, TOK_GROUP, OUT), 1.0, 6.0, ((0, 16), (1, 64)))
    token_target = draw_token_target(jax.random.fold_in(splits[9], 71), 0)
    patches = draw_patches(jax.random.fold_in(splits[9], 71), 0)
    gain = jnp.clip(1.0 + 0.1 * jax.random.normal(splits[3], (D,), jnp.float32), 0.5, 1.5)
    w_down = centred(splits[4], (MERGE_IN, OUT), MERGE_IN ** -0.5, 0.078125, ((1, 16),))
    queries = draw_queries(jax.random.fold_in(splits[9], 71), 0)
    keys = draw_keys(jax.random.fold_in(splits[9], 71), 0)
    values = centred(splits[7], (N_IMG, PATCH_GROUP, D), 1.0, 5.0, ((0, 16), (1, 64)))
    window_ids = jax.vmap(lambda own: jnp.searchsorted(jnp.cumsum(uneven_parts(own, M_DEV // 8, M_DEV, WIN, 2)), jnp.arange(M_DEV), side="right"))(jax.random.split(splits[8], N_IMG * N_SEQ)).reshape((N_IMG, N_SEQ, M_DEV)).astype(jnp.int32)
    return dict(llm_grads=llm_grads, token_target=token_target, patches=patches, gain=gain, w_down=w_down, queries=queries, keys=keys, values=values, window_ids=window_ids)


def group_products(grad_rows, w_down):
    block_width = OUT // N_IMG
    total = jnp.zeros((TOK_GROUP, MERGE_IN), jnp.float32)
    for block_index in range(N_IMG):
        column_block = grad_rows[:, block_index * block_width:(block_index + 1) * block_width]
        weight_block = w_down[:, block_index * block_width:(block_index + 1) * block_width]
        partial_term = jnp.dot(column_block, weight_block.T, preferred_element_type=jnp.float32)
        rounded = lax.optimization_barrier(partial_term.astype(jnp.bfloat16))
        total = total + rounded.astype(jnp.float32)
    return total.astype(jnp.bfloat16)

def norm_backward(token_rows, patch_rows, gain):
    patch_grads = token_rows.reshape(PATCH_GROUP, D).astype(jnp.float32)
    inputs = patch_rows.astype(jnp.float32)
    inverse_rms = lax.rsqrt(lax.optimization_barrier(jnp.mean(inputs * inputs, axis=1, keepdims=True)) + 1e-06)
    normed = inputs * inverse_rms
    gain_part = lax.optimization_barrier(jnp.sum(patch_grads * normed, axis=0))
    scaled = gain[None, :] * patch_grads
    out_grads = inverse_rms * (scaled - normed * lax.optimization_barrier(jnp.mean(scaled * normed, axis=1, keepdims=True)))
    return (out_grads.astype(jnp.bfloat16), gain_part)

def window_backward(operands):
    query_rows, key_rows, value_rows, grad_rows, window_labels = operands
    score_scale = 1.0 / math.sqrt(HEAD_DIM)
    labels = jnp.repeat(window_labels, 4)
    allowed = labels[:, None] == labels[None, :]
    query_heads = query_rows.reshape(P_DEV, HEADS, HEAD_DIM).astype(jnp.float32)
    key_heads = key_rows.reshape(P_DEV, HEADS, HEAD_DIM).astype(jnp.float32)
    value_heads = value_rows.reshape(P_DEV, HEADS, HEAD_DIM).astype(jnp.float32)
    grad_heads = grad_rows.reshape(P_DEV, HEADS, HEAD_DIM).astype(jnp.float32)
    scores = jnp.einsum('phd,qhd->hpq', query_heads, key_heads) * score_scale
    scores = jnp.where(allowed[None, :, :], scores, -jnp.inf)
    peak = lax.optimization_barrier(jnp.max(scores, axis=2, keepdims=True))
    raw_weights = jnp.exp(scores - peak)
    probs = raw_weights / lax.optimization_barrier(jnp.sum(raw_weights, axis=2, keepdims=True))
    probs_bf = probs.astype(jnp.bfloat16).astype(jnp.float32)
    attended = jnp.einsum('hpq,qhd->phd', probs_bf, value_heads)
    row_delta = lax.optimization_barrier(jnp.sum(grad_heads * attended, axis=2))
    prob_grads = jnp.einsum('phd,qhd->hpq', grad_heads, value_heads)
    score_bf = (probs * (prob_grads - jnp.transpose(row_delta)[:, :, None])).astype(jnp.bfloat16).astype(jnp.float32)
    grad_query = jnp.einsum('hpq,qhd->phd', score_bf, key_heads) * score_scale
    grad_key = jnp.einsum('hpq,phd->qhd', score_bf, query_heads) * score_scale
    grad_value = jnp.einsum('hpq,phd->qhd', probs_bf, grad_heads)
    return (grad_query.reshape(P_DEV, D).astype(jnp.bfloat16), grad_key.reshape(P_DEV, D).astype(jnp.bfloat16), grad_value.reshape(P_DEV, D).astype(jnp.bfloat16))

def place_rows(product_rows, target_rows):
    empty = jnp.zeros(product_rows.shape, product_rows.dtype)
    return empty.at[target_rows.astype(jnp.int32)].set(product_rows)

def reference(llm_grads, token_target, patches, gain, w_down, queries, keys, values, window_ids):
    products = lax.map(lambda grad_rows: group_products(grad_rows, w_down), llm_grads)
    merged = jax.vmap(place_rows)(products, token_target)
    out_grads, gain_parts = lax.map(lambda pair: norm_backward(pair[0], pair[1], gain), (merged, patches))
    gain_grad = lax.optimization_barrier(jnp.sum(gain_parts, axis=0)) / math.sqrt(N_IMG * PATCH_GROUP)
    bias_parts = lax.map(lambda grad_rows: lax.optimization_barrier(jnp.sum(grad_rows.astype(jnp.float32), axis=0)), llm_grads)
    bias_grad = lax.optimization_barrier(jnp.sum(bias_parts, axis=0)) / math.sqrt(N_IMG * TOK_GROUP)
    block_count = N_IMG * N_SEQ
    grad_query, grad_key, grad_value = lax.map(window_backward, (queries.reshape(block_count, P_DEV, D), keys.reshape(block_count, P_DEV, D), values.reshape(block_count, P_DEV, D), out_grads.reshape(block_count, P_DEV, D), window_ids.reshape(block_count, M_DEV)))
    return (grad_query.reshape(N_IMG, PATCH_GROUP, D), grad_key.reshape(N_IMG, PATCH_GROUP, D), grad_value.reshape(N_IMG, PATCH_GROUP, D), gain_grad, bias_grad)
```

```python
import functools
import math

import jax
import jax.numpy as jnp
from jax import lax
from jax.experimental import pallas as pl
from jax.experimental.pallas import tpu as pltpu
from jax.sharding import PartitionSpec as P

HEADS = 16
HEAD_DIM = 80


def earlier_equal(labels, order_key):
    same_label = labels[:, None] == labels[None, :]
    earlier = order_key[None, :] < order_key[:, None]
    return jnp.sum(jnp.logical_and(same_label, earlier), axis=1)


def pack_rows(row_values, targets, peer_count, capacity):
    row_count = row_values.shape[0]
    destination = targets // row_count
    local_row = (targets % row_count).astype(jnp.float32).astype(row_values.dtype)
    slot_index = destination * capacity + earlier_equal(
        destination, jnp.arange(row_count, dtype=jnp.int32)
    )
    matches = slot_index[None, :] == jnp.arange(peer_count * capacity, dtype=jnp.int32)[:, None]
    selector = matches.astype(row_values.dtype)
    labelled = jnp.concatenate(
        [row_values, jnp.broadcast_to(local_row[:, None] + 1, (row_count, 128))], axis=1
    )
    return jnp.dot(selector, labelled, preferred_element_type=jnp.float32).astype(row_values.dtype)


def unpack_rows(received, row_count):
    width = received.shape[1] - 128
    labels = received[:, width].astype(jnp.float32).astype(jnp.int32) - 1
    selector = (labels[None, :] == jnp.arange(row_count, dtype=jnp.int32)[:, None]).astype(
        received.dtype
    )
    return jnp.dot(
        selector, received[:, :width], preferred_element_type=jnp.float32
    ).astype(received.dtype)


def project_rows(row_values, w_down):
    columns = lax.all_to_all(row_values, "img", split_axis=1, concat_axis=0, tiled=True)
    bias_part = jnp.sum(columns.astype(jnp.float32), axis=0)
    products = lax.psum_scatter(
        lax.dot_general(
            columns, w_down, (((1,), (1,)), ((), ())), preferred_element_type=jnp.float32
        ).astype(jnp.bfloat16),
        "img",
        scatter_dimension=0,
        tiled=True,
    )
    return products, bias_part


def ring_sum_kernel(
    n_img, n_side, gain_rows, terms, gain_out, bias_out, side_a, side_b, across, send_sem, recv_sem
):
    img = lax.axis_index("img")
    seq = lax.axis_index("seq")
    high = seq // n_side
    low = lax.rem(seq, n_side)

    def along_a(at):
        return (img, at * n_side + low)

    def along_b(at):
        return (img, high * n_side + at)

    def along_img(at):
        return (at, seq)

    stages = (
        (side_a, n_side, high, along_a),
        (side_b, n_side, low, along_b),
        (across, n_img, img, along_img),
    )
    barrier = pltpu.get_barrier_semaphore()
    for _, size, own, peer in stages:
        for step in range(1, size):
            pl.semaphore_signal(
                barrier,
                inc=1,
                device_id=peer(lax.rem(own + step, size)),
                device_id_type=pl.DeviceIdType.MESH,
            )
    pl.semaphore_wait(barrier, 2 * (n_side - 1) + n_img - 1)

    first = 0
    held = terms[...]
    for slots, size, own, peer in stages:
        slots[own] = held
        copies = []
        for step in range(1, size):
            target = lax.rem(own + step, size)
            copy = pltpu.make_async_remote_copy(
                src_ref=slots.at[own],
                dst_ref=slots.at[own],
                send_sem=send_sem.at[first + step],
                recv_sem=recv_sem.at[first + step],
                device_id=peer(target),
                device_id_type=pl.DeviceIdType.MESH,
            )
            copy.start()
            copies.append(copy)
        for step in range(1, size):
            source = lax.rem(own + size - step, size)
            pltpu.make_async_remote_copy(
                src_ref=slots.at[source],
                dst_ref=slots.at[source],
                send_sem=send_sem.at[first + step],
                recv_sem=recv_sem.at[first + step],
                device_id=peer(source),
                device_id_type=pl.DeviceIdType.MESH,
            ).wait_recv()
        for copy in copies:
            copy.wait_send()
        first += size
        if slots is across:
            total = slots[0][:gain_rows]
            for at in range(1, size):
                total += slots[at][:gain_rows]
            gain_out[...] = total
            bias_out[...] = slots[:, gain_rows:, :]
        else:
            held = slots[0]
            for at in range(1, size):
                held += slots[at]


def sum_terms(gain_part, bias_part):
    n_img = lax.axis_size("img")
    n_seq = lax.axis_size("seq")
    n_side = math.isqrt(n_seq)
    gain_rows = -(-gain_part.shape[0] // 1024) * 8
    bias_rows = -(-bias_part.shape[0] // 1024) * 8
    gain_padded = jnp.pad(gain_part, (0, gain_rows * 128 - gain_part.shape[0]))
    bias_padded = jnp.pad(bias_part, (0, bias_rows * 128 - bias_part.shape[0]))
    rows = gain_rows + bias_rows
    terms = jnp.concatenate([gain_padded, bias_padded]).reshape(rows, 128)
    copies = n_img + 2 * n_side
    gain_total, bias_total = pl.pallas_call(
        functools.partial(ring_sum_kernel, n_img, n_side, gain_rows),
        out_shape=(
            jax.ShapeDtypeStruct((gain_rows, 128), jnp.float32),
            jax.ShapeDtypeStruct((n_img, bias_rows, 128), jnp.float32),
        ),
        in_specs=[pl.BlockSpec(memory_space=pltpu.VMEM)],
        out_specs=(
            pl.BlockSpec(memory_space=pltpu.VMEM),
            pl.BlockSpec(memory_space=pltpu.VMEM),
        ),
        scratch_shapes=[
            pltpu.VMEM((n_side, rows, 128), jnp.float32),
            pltpu.VMEM((n_side, rows, 128), jnp.float32),
            pltpu.VMEM((n_img, rows, 128), jnp.float32),
            pltpu.SemaphoreType.DMA((copies,)),
            pltpu.SemaphoreType.DMA((copies,)),
        ],
        compiler_params=pltpu.CompilerParams(collective_id=0, has_side_effects=True),
        name="sum_terms",
    )(terms)
    gain_total = gain_total.reshape(-1)[: gain_part.shape[0]]
    bias_total = bias_total.reshape(n_img, -1)[:, : bias_part.shape[0]].reshape(-1)
    return gain_total, bias_total


def window_backward(query_rows, key_rows, value_rows, grad_rows, window_labels):
    patch_count = query_rows.shape[0]
    patch_width = query_rows.shape[1]
    score_scale = 1.0 / math.sqrt(HEAD_DIM)
    labels = jnp.repeat(window_labels, 4)
    allowed = labels[:, None] == labels[None, :]
    query_heads = query_rows.reshape(patch_count, HEADS, HEAD_DIM)
    key_heads = key_rows.reshape(patch_count, HEADS, HEAD_DIM)
    value_heads = value_rows.reshape(patch_count, HEADS, HEAD_DIM)
    grad_heads = grad_rows.reshape(patch_count, HEADS, HEAD_DIM)
    scores = (
        jnp.einsum("phd,qhd->hpq", query_heads, key_heads, preferred_element_type=jnp.float32)
        * score_scale
    )
    scores = jnp.where(allowed[None, :, :], scores, -jnp.inf)
    peak = jnp.max(scores, axis=2, keepdims=True)
    raw_weights = jnp.exp(scores - peak)
    probs = raw_weights / jnp.sum(raw_weights, axis=2, keepdims=True)
    probs_bf = probs.astype(jnp.bfloat16)
    attended = jnp.einsum("hpq,qhd->phd", probs_bf, value_heads, preferred_element_type=jnp.float32)
    row_delta = jnp.sum(grad_heads.astype(jnp.float32) * attended, axis=2)
    prob_grads = jnp.einsum(
        "phd,qhd->hpq", grad_heads, value_heads, preferred_element_type=jnp.float32
    )
    score_bf = (probs * (prob_grads - jnp.transpose(row_delta)[:, :, None])).astype(jnp.bfloat16)
    grad_query = (
        jnp.einsum("hpq,qhd->phd", score_bf, key_heads, preferred_element_type=jnp.float32)
        * score_scale
    )
    grad_key = (
        jnp.einsum("hpq,phd->qhd", score_bf, query_heads, preferred_element_type=jnp.float32)
        * score_scale
    )
    grad_value = jnp.einsum(
        "hpq,phd->qhd", probs_bf, grad_heads, preferred_element_type=jnp.float32
    )
    return (
        grad_query.reshape(patch_count, patch_width).astype(jnp.bfloat16),
        grad_key.reshape(patch_count, patch_width).astype(jnp.bfloat16),
        grad_value.reshape(patch_count, patch_width).astype(jnp.bfloat16),
    )


def body(llm_grads, token_target, patches, gain, w_down, queries, keys, values, window_ids):
    grad_rows = llm_grads[0]
    targets = token_target[0]
    row_count = grad_rows.shape[0]
    peer_count = lax.axis_size("seq")
    capacity = max(1, 2 * row_count // peer_count)
    products, bias_part = project_rows(grad_rows, w_down)
    packed = pack_rows(products, targets, peer_count, capacity)
    arrived = lax.all_to_all(packed, "seq", split_axis=0, concat_axis=0, tiled=True)
    merged = unpack_rows(arrived, row_count)
    patch_width = patches.shape[2]
    patch_grads = merged.reshape(-1, patch_width).astype(jnp.float32)
    inputs = patches[0].astype(jnp.float32)
    inverse_rms = lax.rsqrt(jnp.mean(inputs * inputs, axis=1, keepdims=True) + 1e-06)
    normed = inputs * inverse_rms
    gain_part = jnp.sum(patch_grads * normed, axis=0)
    gain_total, bias_total = sum_terms(gain_part, bias_part)
    device_count = lax.axis_size("img") * lax.axis_size("seq")
    gain_grad = gain_total / math.sqrt(device_count * inputs.shape[0])
    bias_grad = bias_total / math.sqrt(device_count * row_count)
    scaled = gain[None, :] * patch_grads
    out_grads = (
        inverse_rms * (scaled - normed * jnp.mean(scaled * normed, axis=1, keepdims=True))
    ).astype(jnp.bfloat16)
    grad_query, grad_key, grad_value = window_backward(
        queries[0], keys[0], values[0], out_grads, window_ids[0, 0]
    )
    return (grad_query[None], grad_key[None], grad_value[None], gain_grad, bias_grad)


def solution(mesh):
    return jax.shard_map(
        body,
        mesh=mesh,
        in_specs=(
            P("img", "seq", None),
            P("img", "seq"),
            P("img", "seq", None),
            P(),
            P(None, "img"),
            P("img", "seq", None),
            P("img", "seq", None),
            P("img", "seq", None),
            P("img", "seq", None),
        ),
        out_specs=(P("img", "seq", None), P("img", "seq", None), P("img", "seq", None), P(), P()),
        check_vma=False,
    )
```

```python
import functools
import math

import jax
import jax.numpy as jnp
from jax import lax
from jax.experimental import pallas as pl
from jax.experimental.pallas import tpu as pltpu
from jax.sharding import PartitionSpec as P

HEADS = 16
HEAD_DIM = 80


def earlier_equal(labels, order_key):
    same_label = labels[:, None] == labels[None, :]
    earlier = order_key[None, :] < order_key[:, None]
    return jnp.sum(jnp.logical_and(same_label, earlier), axis=1)


def pack_rows(row_values, targets, peer_count, capacity):
    row_count = row_values.shape[0]
    destination = targets // row_count
    local_row = (targets % row_count).astype(jnp.float32).astype(row_values.dtype)
    slot_index = destination * capacity + earlier_equal(
        destination, jnp.arange(row_count, dtype=jnp.int32)
    )
    matches = slot_index[None, :] == jnp.arange(peer_count * capacity, dtype=jnp.int32)[:, None]
    selector = matches.astype(row_values.dtype)
    labelled = jnp.concatenate(
        [row_values, jnp.broadcast_to(local_row[:, None] + 1, (row_count, 128))], axis=1
    )
    return jnp.dot(selector, labelled, preferred_element_type=jnp.float32).astype(row_values.dtype)


def unpack_rows(received, row_count):
    width = received.shape[1] - 128
    labels = received[:, width].astype(jnp.float32).astype(jnp.int32) - 1
    selector = (labels[None, :] == jnp.arange(row_count, dtype=jnp.int32)[:, None]).astype(
        received.dtype
    )
    return jnp.dot(
        selector, received[:, :width], preferred_element_type=jnp.float32
    ).astype(received.dtype)


CORES = 2
CHUNKS = 5
MESH = pl.DeviceIdType.MESH


def project_kernel(
    n_y,
    grads,
    w_down,
    products,
    bias_part,
    weights,
    columns,
    parts,
    half_out,
    half_in,
    full_out,
    full_in,
    summed,
    swapped,
    weight_sem,
    column_send,
    column_recv,
    relay_send,
    relay_recv,
    ring_send,
    ring_recv,
    swap_send,
    swap_recv,
):
    img = lax.axis_index("img")
    seq = lax.axis_index("seq")
    y = img // CORES
    core = lax.rem(img, CORES)
    other = 1 - core
    hops = n_y // 2
    rows, chip_cols = columns.shape[1], columns.shape[2]
    block = chip_cols // CORES
    half = weights.shape[1]
    width = half // CHUNKS
    side = width // 2
    chip_rows = CORES * rows

    def at_chip(there, which):
        return (there * CORES + which, seq)

    twin = at_chip(y, other)

    barrier = pltpu.get_barrier_semaphore()
    pl.semaphore_signal(barrier, inc=1, device_id=twin, device_id_type=MESH)
    for step in range(1, n_y):
        pl.semaphore_signal(
            barrier,
            inc=1,
            device_id=at_chip(lax.rem(y + step, n_y), core),
            device_id_type=MESH,
        )
    pl.semaphore_wait(barrier, n_y)

    def column_copy(step):
        target = lax.rem(y + step, n_y)
        start = pl.multiple_of(target * chip_cols, chip_cols)
        return pltpu.make_async_remote_copy(
            src_ref=grads.at[:, pl.ds(start, chip_cols)],
            dst_ref=columns.at[y * CORES + core],
            send_sem=column_send.at[step],
            recv_sem=column_recv.at[step],
            device_id=at_chip(target, core),
            device_id_type=MESH,
        )

    def column_arrival(step):
        source = lax.rem(y + n_y - step, n_y)
        return pltpu.make_async_remote_copy(
            src_ref=columns.at[source * CORES + core],
            dst_ref=columns.at[source * CORES + core],
            send_sem=column_send.at[step],
            recv_sem=column_recv.at[step],
            device_id=at_chip(source, core),
            device_id_type=MESH,
        )

    def relay_copy(source):
        slot = source * CORES + core
        return pltpu.make_async_remote_copy(
            src_ref=columns.at[slot],
            dst_ref=columns.at[slot],
            send_sem=relay_send.at[source],
            recv_sem=relay_recv.at[source],
            device_id=twin,
            device_id_type=MESH,
        )

    def relay_arrival(source):
        slot = source * CORES + other
        return pltpu.make_async_remote_copy(
            src_ref=columns.at[slot],
            dst_ref=columns.at[slot],
            send_sem=relay_send.at[source],
            recv_sem=relay_recv.at[source],
            device_id=twin,
            device_id_type=MESH,
        )

    outward = [step for near in range(1, hops + 1) for step in (near, n_y - near)]
    outward = sorted(set(outward), key=lambda step: (-min(step, n_y - step), step))
    for step in outward:
        column_copy(step).start()
    weight_away = pltpu.make_async_remote_copy(
        src_ref=w_down.at[pl.ds(pl.multiple_of(other * half, half), half), :],
        dst_ref=weights.at[core],
        send_sem=weight_sem.at[0],
        recv_sem=weight_sem.at[1],
        device_id=twin,
        device_id_type=MESH,
    )
    weight_away.start()
    weight_here = pltpu.make_async_copy(
        w_down.at[pl.ds(pl.multiple_of(core * half, half), half), :],
        weights.at[core],
        weight_sem.at[2],
    )
    weight_here.start()
    own_start = pl.multiple_of(y * chip_cols, chip_cols)
    own_columns = pltpu.make_async_copy(
        grads.at[:, pl.ds(own_start, chip_cols)],
        columns.at[y * CORES + core],
        weight_sem.at[3],
    )
    own_columns.start()
    own_columns.wait()
    relay_copy(y).start()
    for step in reversed(outward):
        column_arrival(step).wait_recv()
        relay_copy(lax.rem(y + n_y - step, n_y)).start()
    for source in range(n_y):
        relay_arrival(source).wait_recv()
    weight_here.wait()
    pltpu.make_async_remote_copy(
        src_ref=weights.at[other],
        dst_ref=weights.at[other],
        send_sem=weight_sem.at[0],
        recv_sem=weight_sem.at[1],
        device_id=twin,
        device_id_type=MESH,
    ).wait_recv()

    def half_copy(way, n):
        target = lax.rem(y + (1 if way == 0 else n_y - 1), n_y)
        return pltpu.make_async_remote_copy(
            src_ref=half_out.at[way, n],
            dst_ref=half_in.at[way, n],
            send_sem=ring_send.at[way, 0, n],
            recv_sem=ring_recv.at[way, 0, n],
            device_id=at_chip(target, core),
            device_id_type=MESH,
        )

    def full_copy(way, step, n):
        target = lax.rem(y + (1 if way == 0 else n_y - 1), n_y)
        return pltpu.make_async_remote_copy(
            src_ref=full_out.at[way, step - 1, n],
            dst_ref=full_in.at[way, step - 1, n],
            send_sem=ring_send.at[way, step, n],
            recv_sem=ring_recv.at[way, step, n],
            device_id=at_chip(target, core),
            device_id_type=MESH,
        )

    def swap_copy(n):
        return pltpu.make_async_remote_copy(
            src_ref=summed.at[n, other],
            dst_ref=swapped.at[n],
            send_sem=swap_send.at[n],
            recv_sem=swap_recv.at[n],
            device_id=twin,
            device_id_type=MESH,
        )

    def chip_block(there):
        return pl.ds(pl.multiple_of(there * chip_rows, chip_rows), chip_rows)

    over_last = (((1,), (1,)), ((), ()))

    def multiply(n, carry):
        own = pl.ds(pl.multiple_of(n * width, width), width)
        total = None
        for which in range(CORES):
            term = lax.dot_general(
                columns[:, :, which * block : (which + 1) * block].reshape(-1, block),
                weights[which, own, :],
                over_last,
                preferred_element_type=jnp.float32,
            )
            total = term if total is None else total + term
        parts[n] = total
        far = parts[n, chip_block(lax.rem(y + hops, n_y)), :]
        half_out[0, n] = far[:, :side].astype(jnp.bfloat16)
        half_out[1, n] = far[:, side:].astype(jnp.bfloat16)
        half_copy(0, n).start()
        half_copy(1, n).start()
        return carry

    lax.fori_loop(0, CHUNKS, multiply, 0)
    bias_part[...] = jnp.sum(
        columns[...].reshape(-1, chip_cols).astype(jnp.float32), axis=0, keepdims=True
    )

    for step in range(1, hops):

        def pass_on(n, carry):
            for way in range(2):
                distance = hops - step
                there = lax.rem(y + (distance if way == 0 else n_y - distance), n_y)
                mine = parts[n, chip_block(there), :]
                if step == 1:
                    half_copy(way, n).wait_recv()
                    arrived = half_in[way, n].astype(jnp.float32)
                    low, high = mine[:, :side], mine[:, side:]
                    if way == 0:
                        low = low + arrived
                    else:
                        high = high + arrived
                    full_out[way, 0, n, :, :side] = low.astype(jnp.bfloat16)
                    full_out[way, 0, n, :, side:] = high.astype(jnp.bfloat16)
                else:
                    full_copy(way, step - 1, n).wait_recv()
                    arrived = full_in[way, step - 2, n].astype(jnp.float32)
                    full_out[way, step - 1, n] = (mine + arrived).astype(jnp.bfloat16)
                full_copy(way, step, n).start()
            return carry

        lax.fori_loop(0, CHUNKS, pass_on, 0)

    def finish(n, carry):
        total = parts[n, chip_block(y), :]
        for way in range(2):
            full_copy(way, hops - 1, n).wait_recv()
            total = total + full_in[way, hops - 2, n].astype(jnp.float32)
        total = total.astype(jnp.bfloat16)
        for which in range(CORES):
            summed[n, which] = total[which * rows : (which + 1) * rows]
        swap_copy(n).start()
        at = pl.multiple_of(core * half + n * width, width)
        products[:, pl.ds(at, width)] = summed[n, core]
        return carry

    lax.fori_loop(0, CHUNKS, finish, 0)

    def collect(n, carry):
        swap_copy(n).wait_recv()
        at = pl.multiple_of(other * half + n * width, width)
        products[:, pl.ds(at, width)] = swapped[n]
        for way in range(2):
            half_copy(way, n).wait_send()
            for step in range(1, hops):
                full_copy(way, step, n).wait_send()
        swap_copy(n).wait_send()
        return carry

    lax.fori_loop(0, CHUNKS, collect, 0)
    for step in range(1, n_y):
        column_copy(step).wait_send()
    for source in range(n_y):
        relay_copy(source).wait_send()
    weight_away.wait_send()


def project_rows(row_values, w_down):
    n_img = lax.axis_size("img")
    n_y = n_img // CORES
    hops = n_y // 2
    rows, in_width = row_values.shape
    out_width, block = w_down.shape
    half = out_width // CORES
    width = half // CHUNKS
    chip_rows = CORES * rows
    products, bias_sums = pl.pallas_call(
        functools.partial(project_kernel, n_y),
        out_shape=(
            jax.ShapeDtypeStruct((rows, out_width), jnp.bfloat16),
            jax.ShapeDtypeStruct((1, CORES * block), jnp.float32),
        ),
        in_specs=[
            pl.BlockSpec(memory_space=pltpu.VMEM),
            pl.BlockSpec(memory_space=pl.ANY),
        ],
        out_specs=(
            pl.BlockSpec(memory_space=pltpu.VMEM),
            pl.BlockSpec(memory_space=pltpu.VMEM),
        ),
        scratch_shapes=[
            pltpu.VMEM((CORES, half, block), jnp.bfloat16),
            pltpu.VMEM((n_img, rows, CORES * block), jnp.bfloat16),
            pltpu.VMEM((CHUNKS, n_img * rows, width), jnp.float32),
            pltpu.VMEM((2, CHUNKS, chip_rows, width // 2), jnp.bfloat16),
            pltpu.VMEM((2, CHUNKS, chip_rows, width // 2), jnp.bfloat16),
            pltpu.VMEM((2, hops - 1, CHUNKS, chip_rows, width), jnp.bfloat16),
            pltpu.VMEM((2, hops - 1, CHUNKS, chip_rows, width), jnp.bfloat16),
            pltpu.VMEM((CHUNKS, CORES, rows, width), jnp.bfloat16),
            pltpu.VMEM((CHUNKS, rows, width), jnp.bfloat16),
            pltpu.SemaphoreType.DMA((4,)),
            pltpu.SemaphoreType.DMA((n_y,)),
            pltpu.SemaphoreType.DMA((n_y,)),
            pltpu.SemaphoreType.DMA((n_y,)),
            pltpu.SemaphoreType.DMA((n_y,)),
            pltpu.SemaphoreType.DMA((2, hops, CHUNKS)),
            pltpu.SemaphoreType.DMA((2, hops, CHUNKS)),
            pltpu.SemaphoreType.DMA((CHUNKS,)),
            pltpu.SemaphoreType.DMA((CHUNKS,)),
        ],
        compiler_params=pltpu.CompilerParams(
            collective_id=1, has_side_effects=True, vmem_limit_bytes=48 << 20
        ),
        name="project_rows",
    )(row_values, w_down)
    own = lax.rem(lax.axis_index("img"), CORES) * block
    return products, lax.dynamic_slice(bias_sums[0], (own,), (block,))


def ring_sum_kernel(
    n_img, n_side, gain_rows, terms, gain_out, bias_out, side_a, side_b, across, send_sem, recv_sem
):
    img = lax.axis_index("img")
    seq = lax.axis_index("seq")
    high = seq // n_side
    low = lax.rem(seq, n_side)

    def along_a(at):
        return (img, at * n_side + low)

    def along_b(at):
        return (img, high * n_side + at)

    def along_img(at):
        return (at, seq)

    stages = (
        (side_a, n_side, high, along_a),
        (side_b, n_side, low, along_b),
        (across, n_img, img, along_img),
    )
    barrier = pltpu.get_barrier_semaphore()
    for _, size, own, peer in stages:
        for step in range(1, size):
            pl.semaphore_signal(
                barrier,
                inc=1,
                device_id=peer(lax.rem(own + step, size)),
                device_id_type=pl.DeviceIdType.MESH,
            )
    pl.semaphore_wait(barrier, 2 * (n_side - 1) + n_img - 1)

    first = 0
    held = terms[...]
    for slots, size, own, peer in stages:
        slots[own] = held
        copies = []
        for step in range(1, size):
            target = lax.rem(own + step, size)
            copy = pltpu.make_async_remote_copy(
                src_ref=slots.at[own],
                dst_ref=slots.at[own],
                send_sem=send_sem.at[first + step],
                recv_sem=recv_sem.at[first + step],
                device_id=peer(target),
                device_id_type=pl.DeviceIdType.MESH,
            )
            copy.start()
            copies.append(copy)
        for step in range(1, size):
            source = lax.rem(own + size - step, size)
            pltpu.make_async_remote_copy(
                src_ref=slots.at[source],
                dst_ref=slots.at[source],
                send_sem=send_sem.at[first + step],
                recv_sem=recv_sem.at[first + step],
                device_id=peer(source),
                device_id_type=pl.DeviceIdType.MESH,
            ).wait_recv()
        for copy in copies:
            copy.wait_send()
        first += size
        if slots is across:
            total = slots[0][:gain_rows]
            for at in range(1, size):
                total += slots[at][:gain_rows]
            gain_out[...] = total
            bias_out[...] = slots[:, gain_rows:, :]
        else:
            held = slots[0]
            for at in range(1, size):
                held += slots[at]


def sum_terms(gain_part, bias_part):
    n_img = lax.axis_size("img")
    n_seq = lax.axis_size("seq")
    n_side = math.isqrt(n_seq)
    gain_rows = -(-gain_part.shape[0] // 1024) * 8
    bias_rows = -(-bias_part.shape[0] // 1024) * 8
    gain_padded = jnp.pad(gain_part, (0, gain_rows * 128 - gain_part.shape[0]))
    bias_padded = jnp.pad(bias_part, (0, bias_rows * 128 - bias_part.shape[0]))
    rows = gain_rows + bias_rows
    terms = jnp.concatenate([gain_padded, bias_padded]).reshape(rows, 128)
    copies = n_img + 2 * n_side
    gain_total, bias_total = pl.pallas_call(
        functools.partial(ring_sum_kernel, n_img, n_side, gain_rows),
        out_shape=(
            jax.ShapeDtypeStruct((gain_rows, 128), jnp.float32),
            jax.ShapeDtypeStruct((n_img, bias_rows, 128), jnp.float32),
        ),
        in_specs=[pl.BlockSpec(memory_space=pltpu.VMEM)],
        out_specs=(
            pl.BlockSpec(memory_space=pltpu.VMEM),
            pl.BlockSpec(memory_space=pltpu.VMEM),
        ),
        scratch_shapes=[
            pltpu.VMEM((n_side, rows, 128), jnp.float32),
            pltpu.VMEM((n_side, rows, 128), jnp.float32),
            pltpu.VMEM((n_img, rows, 128), jnp.float32),
            pltpu.SemaphoreType.DMA((copies,)),
            pltpu.SemaphoreType.DMA((copies,)),
        ],
        compiler_params=pltpu.CompilerParams(collective_id=0, has_side_effects=True),
        name="sum_terms",
    )(terms)
    gain_total = gain_total.reshape(-1)[: gain_part.shape[0]]
    bias_total = bias_total.reshape(n_img, -1)[:, : bias_part.shape[0]].reshape(-1)
    return gain_total, bias_total


def window_backward(query_rows, key_rows, value_rows, grad_rows, window_labels):
    patch_count = query_rows.shape[0]
    patch_width = query_rows.shape[1]
    score_scale = 1.0 / math.sqrt(HEAD_DIM)
    labels = jnp.repeat(window_labels, 4)
    allowed = labels[:, None] == labels[None, :]
    query_heads = query_rows.reshape(patch_count, HEADS, HEAD_DIM)
    key_heads = key_rows.reshape(patch_count, HEADS, HEAD_DIM)
    value_heads = value_rows.reshape(patch_count, HEADS, HEAD_DIM)
    grad_heads = grad_rows.reshape(patch_count, HEADS, HEAD_DIM)
    scores = (
        jnp.einsum("phd,qhd->hpq", query_heads, key_heads, preferred_element_type=jnp.float32)
        * score_scale
    )
    scores = jnp.where(allowed[None, :, :], scores, -jnp.inf)
    peak = jnp.max(scores, axis=2, keepdims=True)
    raw_weights = jnp.exp(scores - peak)
    probs = raw_weights / jnp.sum(raw_weights, axis=2, keepdims=True)
    probs_bf = probs.astype(jnp.bfloat16)
    attended = jnp.einsum("hpq,qhd->phd", probs_bf, value_heads, preferred_element_type=jnp.float32)
    row_delta = jnp.sum(grad_heads.astype(jnp.float32) * attended, axis=2)
    prob_grads = jnp.einsum(
        "phd,qhd->hpq", grad_heads, value_heads, preferred_element_type=jnp.float32
    )
    score_bf = (probs * (prob_grads - jnp.transpose(row_delta)[:, :, None])).astype(jnp.bfloat16)
    grad_query = (
        jnp.einsum("hpq,qhd->phd", score_bf, key_heads, preferred_element_type=jnp.float32)
        * score_scale
    )
    grad_key = (
        jnp.einsum("hpq,phd->qhd", score_bf, query_heads, preferred_element_type=jnp.float32)
        * score_scale
    )
    grad_value = jnp.einsum(
        "hpq,phd->qhd", probs_bf, grad_heads, preferred_element_type=jnp.float32
    )
    return (
        grad_query.reshape(patch_count, patch_width).astype(jnp.bfloat16),
        grad_key.reshape(patch_count, patch_width).astype(jnp.bfloat16),
        grad_value.reshape(patch_count, patch_width).astype(jnp.bfloat16),
    )


def body(llm_grads, token_target, patches, gain, w_down, queries, keys, values, window_ids):
    grad_rows = llm_grads[0]
    targets = token_target[0]
    row_count = grad_rows.shape[0]
    peer_count = lax.axis_size("seq")
    capacity = max(1, 2 * row_count // peer_count)
    products, bias_part = project_rows(grad_rows, w_down)
    packed = pack_rows(products, targets, peer_count, capacity)
    arrived = lax.all_to_all(packed, "seq", split_axis=0, concat_axis=0, tiled=True)
    merged = unpack_rows(arrived, row_count)
    patch_width = patches.shape[2]
    patch_grads = merged.reshape(-1, patch_width).astype(jnp.float32)
    inputs = patches[0].astype(jnp.float32)
    inverse_rms = lax.rsqrt(jnp.mean(inputs * inputs, axis=1, keepdims=True) + 1e-06)
    normed = inputs * inverse_rms
    gain_part = jnp.sum(patch_grads * normed, axis=0)
    gain_total, bias_total = sum_terms(gain_part, bias_part)
    device_count = lax.axis_size("img") * lax.axis_size("seq")
    gain_grad = gain_total / math.sqrt(device_count * inputs.shape[0])
    bias_grad = bias_total / math.sqrt(device_count * row_count)
    scaled = gain[None, :] * patch_grads
    out_grads = (
        inverse_rms * (scaled - normed * jnp.mean(scaled * normed, axis=1, keepdims=True))
    ).astype(jnp.bfloat16)
    grad_query, grad_key, grad_value = window_backward(
        queries[0], keys[0], values[0], out_grads, window_ids[0, 0]
    )
    return (grad_query[None], grad_key[None], grad_value[None], gain_grad, bias_grad)


def solution(mesh):
    return jax.shard_map(
        body,
        mesh=mesh,
        in_specs=(
            P("img", "seq", None),
            P("img", "seq"),
            P("img", "seq", None),
            P(),
            P(None, "img"),
            P("img", "seq", None),
            P("img", "seq", None),
            P("img", "seq", None),
            P("img", "seq", None),
        ),
        out_specs=(P("img", "seq", None), P("img", "seq", None), P("img", "seq", None), P(), P()),
        check_vma=False,
    )
```

```python
import functools
import math

import jax
import jax.numpy as jnp
from jax import lax
from jax.experimental import pallas as pl
from jax.experimental.pallas import tpu as pltpu
from jax.sharding import PartitionSpec as P

HEADS = 16
HEAD_DIM = 80


FOLD = 8


def route_tables(targets, peer_count):
    row_count = targets.shape[0]
    destination = targets // row_count
    local_row = targets % row_count
    matches = destination[None, :] == jnp.arange(peer_count, dtype=jnp.int32)[:, None]
    labels = jnp.sum(jnp.where(matches, local_row[None, :] + 1, 0), axis=1)
    slot_of = lax.broadcasted_iota(jnp.int32, (peer_count * FOLD, FOLD * row_count), 0)
    fold_of = lax.broadcasted_iota(jnp.int32, (peer_count * FOLD, FOLD * row_count), 1)
    selector = jnp.logical_and(
        slot_of // FOLD == jnp.tile(destination, FOLD)[None, :],
        slot_of % FOLD == fold_of // row_count,
    ).astype(jnp.bfloat16)
    labels = jnp.broadcast_to(labels.astype(jnp.int32)[:, None, None], (peer_count, 1, 128))
    return selector, labels


def place_patches(arrived, labels, row_count, patches_per_row):
    peer_count, _, piece = arrived.shape
    pieces = FOLD // patches_per_row
    flat = arrived.reshape(peer_count * FOLD, piece)
    wanted = (labels[:, None] - 1) * FOLD + jnp.arange(FOLD, dtype=jnp.int32)[None, :]
    wanted = wanted.reshape(-1)
    patch = jnp.arange(row_count * patches_per_row, dtype=jnp.int32)
    columns = []
    for at in range(pieces):
        selector = (wanted[None, :] == (patch * pieces + at)[:, None]).astype(flat.dtype)
        columns.append(jnp.dot(selector, flat, preferred_element_type=jnp.float32))
    return jnp.concatenate(columns, axis=1)


CORES = 2
CHUNKS = 5
MESH = pl.DeviceIdType.MESH


def project_kernel(
    n_y,
    n_side,
    grads,
    w_down,
    selector,
    labels,
    arrived_out,
    labels_out,
    bias_part,
    products,
    packed,
    arrived,
    label_slots,
    weights,
    columns,
    parts,
    half_out,
    half_in,
    full_out,
    full_in,
    summed,
    swapped,
    weight_sem,
    column_send,
    column_recv,
    relay_send,
    relay_recv,
    ring_send,
    ring_recv,
    swap_send,
    swap_recv,
    label_send,
    label_recv,
    route_send,
    route_recv,
):
    img = lax.axis_index("img")
    seq = lax.axis_index("seq")
    y = img // CORES
    core = lax.rem(img, CORES)
    other = 1 - core
    hops = n_y // 2
    rows, chip_cols = columns.shape[1], columns.shape[2]
    block = chip_cols // CORES
    half = weights.shape[1]
    width = half // CHUNKS
    side = width // 2
    chip_rows = CORES * rows

    def at_chip(there, which):
        return (there * CORES + which, seq)

    twin = at_chip(y, other)
    n_seq = n_side * n_side
    high = seq // n_side
    low = lax.rem(seq, n_side)

    def ahead(step):
        return (
            lax.rem(high + step // n_side, n_side) * n_side
            + lax.rem(low + lax.rem(step, n_side), n_side)
        )

    def behind(step):
        return (
            lax.rem(high + n_side - step // n_side, n_side) * n_side
            + lax.rem(low + n_side - lax.rem(step, n_side), n_side)
        )

    def label_copy(step):
        target = ahead(step)
        return pltpu.make_async_remote_copy(
            src_ref=labels.at[target],
            dst_ref=label_slots.at[seq],
            send_sem=label_send.at[step],
            recv_sem=label_recv.at[step],
            device_id=(img, target),
            device_id_type=MESH,
        )

    def route_copy(step):
        target = ahead(step)
        return pltpu.make_async_remote_copy(
            src_ref=packed.at[target],
            dst_ref=arrived.at[seq],
            send_sem=route_send.at[step],
            recv_sem=route_recv.at[step],
            device_id=(img, target),
            device_id_type=MESH,
        )

    def label_arrival(step):
        source = behind(step)
        return pltpu.make_async_remote_copy(
            src_ref=labels.at[source],
            dst_ref=label_slots.at[source],
            send_sem=label_send.at[step],
            recv_sem=label_recv.at[step],
            device_id=(img, source),
            device_id_type=MESH,
        )

    def route_arrival(step):
        source = behind(step)
        return pltpu.make_async_remote_copy(
            src_ref=packed.at[source],
            dst_ref=arrived.at[source],
            send_sem=route_send.at[step],
            recv_sem=route_recv.at[step],
            device_id=(img, source),
            device_id_type=MESH,
        )

    barrier = pltpu.get_barrier_semaphore()
    pl.semaphore_signal(barrier, inc=1, device_id=twin, device_id_type=MESH)
    for step in range(1, n_y):
        pl.semaphore_signal(
            barrier,
            inc=1,
            device_id=at_chip(lax.rem(y + step, n_y), core),
            device_id_type=MESH,
        )

    def greet(step, carry):
        pl.semaphore_signal(barrier, inc=1, device_id=(img, ahead(step)), device_id_type=MESH)
        return carry

    lax.fori_loop(1, n_seq, greet, 0)
    pl.semaphore_wait(barrier, n_y + n_seq - 1)

    def column_copy(step):
        target = lax.rem(y + step, n_y)
        start = pl.multiple_of(target * chip_cols, chip_cols)
        return pltpu.make_async_remote_copy(
            src_ref=grads.at[:, pl.ds(start, chip_cols)],
            dst_ref=columns.at[y * CORES + core],
            send_sem=column_send.at[step],
            recv_sem=column_recv.at[step],
            device_id=at_chip(target, core),
            device_id_type=MESH,
        )

    def column_arrival(step):
        source = lax.rem(y + n_y - step, n_y)
        return pltpu.make_async_remote_copy(
            src_ref=columns.at[source * CORES + core],
            dst_ref=columns.at[source * CORES + core],
            send_sem=column_send.at[step],
            recv_sem=column_recv.at[step],
            device_id=at_chip(source, core),
            device_id_type=MESH,
        )

    def relay_copy(source):
        slot = source * CORES + core
        return pltpu.make_async_remote_copy(
            src_ref=columns.at[slot],
            dst_ref=columns.at[slot],
            send_sem=relay_send.at[source],
            recv_sem=relay_recv.at[source],
            device_id=twin,
            device_id_type=MESH,
        )

    def relay_arrival(source):
        slot = source * CORES + other
        return pltpu.make_async_remote_copy(
            src_ref=columns.at[slot],
            dst_ref=columns.at[slot],
            send_sem=relay_send.at[source],
            recv_sem=relay_recv.at[source],
            device_id=twin,
            device_id_type=MESH,
        )

    outward = [step for near in range(1, hops + 1) for step in (near, n_y - near)]
    outward = sorted(set(outward), key=lambda step: (-min(step, n_y - step), step))
    for step in outward:
        column_copy(step).start()
    weight_away = pltpu.make_async_remote_copy(
        src_ref=w_down.at[pl.ds(pl.multiple_of(other * half, half), half), :],
        dst_ref=weights.at[core],
        send_sem=weight_sem.at[0],
        recv_sem=weight_sem.at[1],
        device_id=twin,
        device_id_type=MESH,
    )
    weight_away.start()
    weight_here = pltpu.make_async_copy(
        w_down.at[pl.ds(pl.multiple_of(core * half, half), half), :],
        weights.at[core],
        weight_sem.at[2],
    )
    weight_here.start()
    own_start = pl.multiple_of(y * chip_cols, chip_cols)
    own_columns = pltpu.make_async_copy(
        grads.at[:, pl.ds(own_start, chip_cols)],
        columns.at[y * CORES + core],
        weight_sem.at[3],
    )
    own_columns.start()

    def send_label(step, carry):
        label_copy(step).start()
        return carry

    lax.fori_loop(1, n_seq, send_label, 0)
    label_slots[seq] = labels[seq]
    own_columns.wait()
    relay_copy(y).start()
    for step in reversed(outward):
        column_arrival(step).wait_recv()
        relay_copy(lax.rem(y + n_y - step, n_y)).start()
    for source in range(n_y):
        relay_arrival(source).wait_recv()
    weight_here.wait()
    pltpu.make_async_remote_copy(
        src_ref=weights.at[other],
        dst_ref=weights.at[other],
        send_sem=weight_sem.at[0],
        recv_sem=weight_sem.at[1],
        device_id=twin,
        device_id_type=MESH,
    ).wait_recv()

    def half_copy(way, n):
        target = lax.rem(y + (1 if way == 0 else n_y - 1), n_y)
        return pltpu.make_async_remote_copy(
            src_ref=half_out.at[way, n],
            dst_ref=half_in.at[way, n],
            send_sem=ring_send.at[way, 0, n],
            recv_sem=ring_recv.at[way, 0, n],
            device_id=at_chip(target, core),
            device_id_type=MESH,
        )

    def full_copy(way, step, n):
        target = lax.rem(y + (1 if way == 0 else n_y - 1), n_y)
        return pltpu.make_async_remote_copy(
            src_ref=full_out.at[way, step - 1, n],
            dst_ref=full_in.at[way, step - 1, n],
            send_sem=ring_send.at[way, step, n],
            recv_sem=ring_recv.at[way, step, n],
            device_id=at_chip(target, core),
            device_id_type=MESH,
        )

    def swap_copy(n):
        return pltpu.make_async_remote_copy(
            src_ref=summed.at[n, other],
            dst_ref=swapped.at[n],
            send_sem=swap_send.at[n],
            recv_sem=swap_recv.at[n],
            device_id=twin,
            device_id_type=MESH,
        )

    def chip_block(there):
        return pl.ds(pl.multiple_of(there * chip_rows, chip_rows), chip_rows)

    over_last = (((1,), (1,)), ((), ()))

    def multiply(n, carry):
        own = pl.ds(pl.multiple_of(n * width, width), width)
        total = None
        for which in range(CORES):
            term = lax.dot_general(
                columns[:, :, which * block : (which + 1) * block].reshape(-1, block),
                weights[which, own, :],
                over_last,
                preferred_element_type=jnp.float32,
            )
            total = term if total is None else total + term
        parts[n] = total
        far = parts[n, chip_block(lax.rem(y + hops, n_y)), :]
        half_out[0, n] = far[:, :side].astype(jnp.bfloat16)
        half_out[1, n] = far[:, side:].astype(jnp.bfloat16)
        half_copy(0, n).start()
        half_copy(1, n).start()
        return carry

    lax.fori_loop(0, CHUNKS, multiply, 0)
    bias_part[...] = jnp.sum(
        columns[...].reshape(-1, chip_cols).astype(jnp.float32), axis=0, keepdims=True
    )

    for step in range(1, hops):

        def pass_on(n, carry):
            for way in range(2):
                distance = hops - step
                there = lax.rem(y + (distance if way == 0 else n_y - distance), n_y)
                mine = parts[n, chip_block(there), :]
                if step == 1:
                    half_copy(way, n).wait_recv()
                    arrived = half_in[way, n].astype(jnp.float32)
                    low, high = mine[:, :side], mine[:, side:]
                    if way == 0:
                        low = low + arrived
                    else:
                        high = high + arrived
                    full_out[way, 0, n, :, :side] = low.astype(jnp.bfloat16)
                    full_out[way, 0, n, :, side:] = high.astype(jnp.bfloat16)
                else:
                    full_copy(way, step - 1, n).wait_recv()
                    arrived = full_in[way, step - 2, n].astype(jnp.float32)
                    full_out[way, step - 1, n] = (mine + arrived).astype(jnp.bfloat16)
                full_copy(way, step, n).start()
            return carry

        lax.fori_loop(0, CHUNKS, pass_on, 0)

    def finish(n, carry):
        total = parts[n, chip_block(y), :]
        for way in range(2):
            full_copy(way, hops - 1, n).wait_recv()
            total = total + full_in[way, hops - 2, n].astype(jnp.float32)
        total = total.astype(jnp.bfloat16)
        for which in range(CORES):
            summed[n, which] = total[which * rows : (which + 1) * rows]
        swap_copy(n).start()
        at = pl.multiple_of(core * half + n * width, width)
        products[:, pl.ds(at, width)] = summed[n, core]
        return carry

    lax.fori_loop(0, CHUNKS, finish, 0)

    def collect(n, carry):
        swap_copy(n).wait_recv()
        at = pl.multiple_of(other * half + n * width, width)
        products[:, pl.ds(at, width)] = swapped[n]
        for way in range(2):
            half_copy(way, n).wait_send()
            for step in range(1, hops):
                full_copy(way, step, n).wait_send()
        swap_copy(n).wait_send()
        return carry

    lax.fori_loop(0, CHUNKS, collect, 0)

    piece = packed.shape[2]
    folded = jnp.concatenate(
        [products[:, at * piece : (at + 1) * piece] for at in range(FOLD)], axis=0
    )
    packed[...] = (
        jnp.dot(selector[...], folded, preferred_element_type=jnp.float32)
        .reshape(n_seq, FOLD, piece)
        .astype(jnp.bfloat16)
    )

    def send_row(step, carry):
        route_copy(step).start()
        return carry

    lax.fori_loop(1, n_seq, send_row, 0)
    arrived[seq] = packed[seq]
    for step in range(1, n_y):
        column_copy(step).wait_send()
    for source in range(n_y):
        relay_copy(source).wait_send()
    weight_away.wait_send()

    def settle(step, carry):
        label_arrival(step).wait_recv()
        label_copy(step).wait_send()
        route_arrival(step).wait_recv()
        route_copy(step).wait_send()
        return carry

    lax.fori_loop(1, n_seq, settle, 0)
    arrived_out[...] = arrived[...]
    labels_out[...] = label_slots[...]


def project_rows(row_values, w_down, selector, labels):
    n_img = lax.axis_size("img")
    n_seq = lax.axis_size("seq")
    n_side = math.isqrt(n_seq)
    n_y = n_img // CORES
    hops = n_y // 2
    rows, in_width = row_values.shape
    out_width, block = w_down.shape
    half = out_width // CORES
    width = half // CHUNKS
    chip_rows = CORES * rows
    arrived, arrived_labels, bias_sums = pl.pallas_call(
        functools.partial(project_kernel, n_y, n_side),
        out_shape=(
            jax.ShapeDtypeStruct((n_seq, FOLD, out_width // FOLD), jnp.bfloat16),
            jax.ShapeDtypeStruct((n_seq, 1, 128), jnp.int32),
            jax.ShapeDtypeStruct((1, CORES * block), jnp.float32),
        ),
        in_specs=[
            pl.BlockSpec(memory_space=pltpu.VMEM),
            pl.BlockSpec(memory_space=pltpu.HBM),
            pl.BlockSpec(memory_space=pltpu.VMEM),
            pl.BlockSpec(memory_space=pltpu.VMEM),
        ],
        out_specs=(
            pl.BlockSpec(memory_space=pltpu.VMEM),
            pl.BlockSpec(memory_space=pltpu.VMEM),
            pl.BlockSpec(memory_space=pltpu.VMEM),
        ),
        scratch_shapes=[
            pltpu.VMEM((rows, out_width), jnp.bfloat16),
            pltpu.VMEM((n_seq, FOLD, out_width // FOLD), jnp.bfloat16),
            pltpu.VMEM((n_seq, FOLD, out_width // FOLD), jnp.bfloat16),
            pltpu.VMEM((n_seq, 1, 128), jnp.int32),
            pltpu.VMEM((CORES, half, block), jnp.bfloat16),
            pltpu.VMEM((n_img, rows, CORES * block), jnp.bfloat16),
            pltpu.VMEM((CHUNKS, n_img * rows, width), jnp.float32),
            pltpu.VMEM((2, CHUNKS, chip_rows, width // 2), jnp.bfloat16),
            pltpu.VMEM((2, CHUNKS, chip_rows, width // 2), jnp.bfloat16),
            pltpu.VMEM((2, hops - 1, CHUNKS, chip_rows, width), jnp.bfloat16),
            pltpu.VMEM((2, hops - 1, CHUNKS, chip_rows, width), jnp.bfloat16),
            pltpu.VMEM((CHUNKS, CORES, rows, width), jnp.bfloat16),
            pltpu.VMEM((CHUNKS, rows, width), jnp.bfloat16),
            pltpu.SemaphoreType.DMA((4,)),
            pltpu.SemaphoreType.DMA((n_y,)),
            pltpu.SemaphoreType.DMA((n_y,)),
            pltpu.SemaphoreType.DMA((n_y,)),
            pltpu.SemaphoreType.DMA((n_y,)),
            pltpu.SemaphoreType.DMA((2, hops, CHUNKS)),
            pltpu.SemaphoreType.DMA((2, hops, CHUNKS)),
            pltpu.SemaphoreType.DMA((CHUNKS,)),
            pltpu.SemaphoreType.DMA((CHUNKS,)),
            pltpu.SemaphoreType.DMA((n_seq,)),
            pltpu.SemaphoreType.DMA((n_seq,)),
            pltpu.SemaphoreType.DMA((n_seq,)),
            pltpu.SemaphoreType.DMA((n_seq,)),
        ],
        compiler_params=pltpu.CompilerParams(
            collective_id=1, has_side_effects=True, vmem_limit_bytes=48 << 20
        ),
        name="project_rows",
    )(row_values, w_down, selector, labels)
    own = lax.rem(lax.axis_index("img"), CORES) * block
    bias_part = lax.dynamic_slice(bias_sums[0], (own,), (block,))
    return arrived, arrived_labels[:, 0, 0], bias_part


def ring_sum_kernel(
    n_img, n_side, gain_rows, terms, gain_out, bias_out, side_a, side_b, across, send_sem, recv_sem
):
    img = lax.axis_index("img")
    seq = lax.axis_index("seq")
    high = seq // n_side
    low = lax.rem(seq, n_side)

    def along_a(at):
        return (img, at * n_side + low)

    def along_b(at):
        return (img, high * n_side + at)

    def along_img(at):
        return (at, seq)

    stages = (
        (side_a, n_side, high, along_a),
        (side_b, n_side, low, along_b),
        (across, n_img, img, along_img),
    )
    barrier = pltpu.get_barrier_semaphore()
    for _, size, own, peer in stages:
        for step in range(1, size):
            pl.semaphore_signal(
                barrier,
                inc=1,
                device_id=peer(lax.rem(own + step, size)),
                device_id_type=pl.DeviceIdType.MESH,
            )
    pl.semaphore_wait(barrier, 2 * (n_side - 1) + n_img - 1)

    first = 0
    held = terms[...]
    for slots, size, own, peer in stages:
        slots[own] = held
        copies = []
        for step in range(1, size):
            target = lax.rem(own + step, size)
            copy = pltpu.make_async_remote_copy(
                src_ref=slots.at[own],
                dst_ref=slots.at[own],
                send_sem=send_sem.at[first + step],
                recv_sem=recv_sem.at[first + step],
                device_id=peer(target),
                device_id_type=pl.DeviceIdType.MESH,
            )
            copy.start()
            copies.append(copy)
        for step in range(1, size):
            source = lax.rem(own + size - step, size)
            pltpu.make_async_remote_copy(
                src_ref=slots.at[source],
                dst_ref=slots.at[source],
                send_sem=send_sem.at[first + step],
                recv_sem=recv_sem.at[first + step],
                device_id=peer(source),
                device_id_type=pl.DeviceIdType.MESH,
            ).wait_recv()
        for copy in copies:
            copy.wait_send()
        first += size
        if slots is across:
            total = slots[0][:gain_rows]
            for at in range(1, size):
                total += slots[at][:gain_rows]
            gain_out[...] = total
            bias_out[...] = slots[:, gain_rows:, :]
        else:
            held = slots[0]
            for at in range(1, size):
                held += slots[at]


def sum_terms(gain_part, bias_part):
    n_img = lax.axis_size("img")
    n_seq = lax.axis_size("seq")
    n_side = math.isqrt(n_seq)
    gain_rows = -(-gain_part.shape[0] // 1024) * 8
    bias_rows = -(-bias_part.shape[0] // 1024) * 8
    gain_padded = jnp.pad(gain_part, (0, gain_rows * 128 - gain_part.shape[0]))
    bias_padded = jnp.pad(bias_part, (0, bias_rows * 128 - bias_part.shape[0]))
    rows = gain_rows + bias_rows
    terms = jnp.concatenate([gain_padded, bias_padded]).reshape(rows, 128)
    copies = n_img + 2 * n_side
    gain_total, bias_total = pl.pallas_call(
        functools.partial(ring_sum_kernel, n_img, n_side, gain_rows),
        out_shape=(
            jax.ShapeDtypeStruct((gain_rows, 128), jnp.float32),
            jax.ShapeDtypeStruct((n_img, bias_rows, 128), jnp.float32),
        ),
        in_specs=[pl.BlockSpec(memory_space=pltpu.VMEM)],
        out_specs=(
            pl.BlockSpec(memory_space=pltpu.VMEM),
            pl.BlockSpec(memory_space=pltpu.VMEM),
        ),
        scratch_shapes=[
            pltpu.VMEM((n_side, rows, 128), jnp.float32),
            pltpu.VMEM((n_side, rows, 128), jnp.float32),
            pltpu.VMEM((n_img, rows, 128), jnp.float32),
            pltpu.SemaphoreType.DMA((copies,)),
            pltpu.SemaphoreType.DMA((copies,)),
        ],
        compiler_params=pltpu.CompilerParams(collective_id=0, has_side_effects=True),
        name="sum_terms",
    )(terms)
    gain_total = gain_total.reshape(-1)[: gain_part.shape[0]]
    bias_total = bias_total.reshape(n_img, -1)[:, : bias_part.shape[0]].reshape(-1)
    return gain_total, bias_total


def window_backward(query_rows, key_rows, value_rows, grad_rows, window_labels):
    patch_count = query_rows.shape[0]
    patch_width = query_rows.shape[1]
    score_scale = 1.0 / math.sqrt(HEAD_DIM)
    labels = jnp.repeat(window_labels, 4)
    allowed = labels[:, None] == labels[None, :]
    query_heads = query_rows.reshape(patch_count, HEADS, HEAD_DIM)
    key_heads = key_rows.reshape(patch_count, HEADS, HEAD_DIM)
    value_heads = value_rows.reshape(patch_count, HEADS, HEAD_DIM)
    grad_heads = grad_rows.reshape(patch_count, HEADS, HEAD_DIM)
    scores = (
        jnp.einsum("phd,qhd->hpq", query_heads, key_heads, preferred_element_type=jnp.float32)
        * score_scale
    )
    scores = jnp.where(allowed[None, :, :], scores, -jnp.inf)
    peak = jnp.max(scores, axis=2, keepdims=True)
    raw_weights = jnp.exp(scores - peak)
    probs = raw_weights / jnp.sum(raw_weights, axis=2, keepdims=True)
    probs_bf = probs.astype(jnp.bfloat16)
    attended = jnp.einsum("hpq,qhd->phd", probs_bf, value_heads, preferred_element_type=jnp.float32)
    row_delta = jnp.sum(grad_heads.astype(jnp.float32) * attended, axis=2)
    prob_grads = jnp.einsum(
        "phd,qhd->hpq", grad_heads, value_heads, preferred_element_type=jnp.float32
    )
    score_bf = (probs * (prob_grads - jnp.transpose(row_delta)[:, :, None])).astype(jnp.bfloat16)
    grad_query = (
        jnp.einsum("hpq,qhd->phd", score_bf, key_heads, preferred_element_type=jnp.float32)
        * score_scale
    )
    grad_key = (
        jnp.einsum("hpq,phd->qhd", score_bf, query_heads, preferred_element_type=jnp.float32)
        * score_scale
    )
    grad_value = jnp.einsum(
        "hpq,phd->qhd", probs_bf, grad_heads, preferred_element_type=jnp.float32
    )
    return (
        grad_query.reshape(patch_count, patch_width).astype(jnp.bfloat16),
        grad_key.reshape(patch_count, patch_width).astype(jnp.bfloat16),
        grad_value.reshape(patch_count, patch_width).astype(jnp.bfloat16),
    )


def body(llm_grads, token_target, patches, gain, w_down, queries, keys, values, window_ids):
    grad_rows = llm_grads[0]
    targets = token_target[0]
    row_count = grad_rows.shape[0]
    peer_count = lax.axis_size("seq")
    patch_width = patches.shape[2]
    selector, labels = route_tables(targets, peer_count)
    arrived, arrived_labels, bias_part = project_rows(grad_rows, w_down, selector, labels)
    patch_grads = place_patches(
        arrived, arrived_labels, row_count, w_down.shape[0] // patch_width
    )
    inputs = patches[0].astype(jnp.float32)
    inverse_rms = lax.rsqrt(jnp.mean(inputs * inputs, axis=1, keepdims=True) + 1e-06)
    normed = inputs * inverse_rms
    gain_part = jnp.sum(patch_grads * normed, axis=0)
    gain_total, bias_total = sum_terms(gain_part, bias_part)
    device_count = lax.axis_size("img") * lax.axis_size("seq")
    gain_grad = gain_total / math.sqrt(device_count * inputs.shape[0])
    bias_grad = bias_total / math.sqrt(device_count * row_count)
    scaled = gain[None, :] * patch_grads
    out_grads = (
        inverse_rms * (scaled - normed * jnp.mean(scaled * normed, axis=1, keepdims=True))
    ).astype(jnp.bfloat16)
    grad_query, grad_key, grad_value = window_backward(
        queries[0], keys[0], values[0], out_grads, window_ids[0, 0]
    )
    return (grad_query[None], grad_key[None], grad_value[None], gain_grad, bias_grad)


def solution(mesh):
    return jax.shard_map(
        body,
        mesh=mesh,
        in_specs=(
            P("img", "seq", None),
            P("img", "seq"),
            P("img", "seq", None),
            P(),
            P(None, "img"),
            P("img", "seq", None),
            P("img", "seq", None),
            P("img", "seq", None),
            P("img", "seq", None),
        ),
        out_specs=(P("img", "seq", None), P("img", "seq", None), P("img", "seq", None), P(), P()),
        check_vma=False,
    )
```
